512 devices in a mesh: grp: 8 (over z_lo, core), cell: 64 (over x, z_hi, y).
Axes of the slice: x: 4, y: 8, z: 8 (z_hi: 2, z_lo: 4; z = z_hi * 4 + z_lo), core: 2. Of those that a mesh axis runs over, the one named last changes fastest.
Arguments:
- row_embed: bfloat16 [8, 128, 64, 512], P('grp', 'cell'), may hold values from -16 to 16
- cotangent: bfloat16 [8, 128, 64, 512], P('grp', 'cell'), may hold values from -16 to 16
- w_qkv: bfloat16 [1536, 512], replicated, may hold values from -0.25 to 0.25
- w_out: bfloat16 [512, 512], replicated, may hold values from -0.25 to 0.25
- treat_vec: float32 [512], replicated, may hold values from -3 to 3
- is_train: int32 [8, 128], P('grp'), may hold values 0 or 1
- treated: int32 [8, 128], P('grp'), may hold values 0 or 1
- block_pattern: int32 [4, 4], replicated, may hold values 0 or 1
Outputs:
- out: bfloat16 [8, 128, 64, 512], P('grp', 'cell')
- grad_input: bfloat16 [8, 128, 64, 512], P('grp', 'cell')
- weight_grads: float32 [2048, 512], P('cell')
The draws below stay inside these ranges and needn't reach their ends.
All inputs are finite; a program needn't handle non-finite values. No bound on the sum of `is_train` or of `treated` on one device may be relied on, other than what follows from the above.
Results may differ from the reference program's by a relative error of at most 0.014.
The reference program's roundings to bfloat16 on the way (of `shifted`, `projected`, `prob_b`, `attended`, `grad_attended`, `grad_score` and `grad_projected`) count: a program that leaves them out, or rounds other values in their place, can miss the bound.
Values may be sent and summed in bfloat16 or wider, within the bound.
No kernel may reach another device: no remote copies, remote signals or barrier semaphores. Data moves between devices by JAX's collectives and lax.ppermute only.
A program may use at most 64 MiB of HBM per device.

```python
import math
import jax
import jax.numpy as jnp
from jax import lax

D = 512
HEADS = 8
HD = 64
FEATS = 64
ROWS = 128
BLK = 32
NBLK = 4
GROUPS = 8


def draw_row_embed(key, part):
    key_base = jax.random.fold_in(key, 0)
    shape = (GROUPS, ROWS, FEATS, D)
    result = jax.random.normal(key_base, shape, jnp.float32)
    return jnp.clip(result, -16.0, 16.0).astype(jnp.bfloat16)


def touch_ends(values, stream_key, least, high):
    longest = values.shape.index(max(values.shape))
    spots = []
    for shift in (0, 1):
        where = [jax.random.randint(jax.random.fold_in(stream_key, axis), (), 0, length) for axis, length in enumerate(values.shape)]
        where[longest] = (where[longest] + shift) % values.shape[longest]
        spots.append(tuple(where))
    return values.at[spots[0]].set(least).at[spots[1]].set(high)


def with_spikes(array, stream_key, source, target, shards_of, factor):
    owner, partner = [(jnp.arange(array.shape[axis_at]) // (array.shape[axis_at] // shards_of)).reshape([-1 if axis == axis_at else 1 for axis in range(array.ndim)]) for axis_at in (source, target)]
    chosen = jax.random.permutation(stream_key, shards_of)[partner]
    strong = (owner == chosen) | (owner == (partner + shards_of // 2) % shards_of)
    return jnp.where(strong, factor * array, array)


def levels(rng, extent, pieces, smallest, largest):
    def one(position, parts):
        draws = jax.random.uniform(jax.random.fold_in(jax.random.fold_in(rng, 6), position), (parts,), jnp.float32, smallest / len(pieces), largest / len(pieces))
        return jnp.repeat(jnp.exp(draws), extent[position] // parts).reshape((-1,) + (1,) * (len(extent) - position - 1))

    level = one(*pieces[0])
    for cut in pieces[1:]:
        level = level * one(*cut)
    return level


def scatter_about(own_key, shape, spread, reach, shards=(), held_as=jnp.bfloat16):
    factor_of = levels(own_key, shape, shards, -0.22, 0.18) if shards else 1.0
    entries = jax.random.normal(own_key, shape, jnp.float32) * spread * factor_of
    return jnp.minimum(jnp.maximum(entries, -reach), reach).astype(held_as)


def bell_draw_with(rng, shape, deviation, bound, shards, heavy, held_as=jnp.bfloat16):
    entries = deviation * jax.random.normal(rng, shape, jnp.float32)
    if shards:
        entries = entries * levels(rng, shape, shards, -0.22, 0.18)
    return jnp.clip(with_spikes(entries, jax.random.fold_in(rng, 3), *heavy), -bound, bound).astype(held_as)


def setup_inputs(seed: int = 0) -> dict:
    keys = jax.random.split(jax.random.key(seed), 9)
    row_embed = draw_row_embed(jax.random.fold_in(keys[8], 71), 0)
    cotangent = bell_draw_with(keys[1], (GROUPS, ROWS, FEATS, D), 1.0, 16.0, ((0, 8), (1, 64)), (1, 3, 64, 4.0))
    w_qkv = scatter_about(keys[2], (3 * D, D), D ** -0.5, 0.25)
    w_out = scatter_about(keys[3], (D, D), D ** -0.5, 0.25)
    treat_vec = scatter_about(keys[4], (D,), 0.5, 3.0, (), jnp.float32)
    is_train = touch_ends((jax.random.randint(keys[5], (GROUPS, ROWS), 0, 3) < 2).astype(jnp.int32), jax.random.fold_in(keys[5], 1), 0, 1)
    treated = touch_ends((jax.random.randint(keys[6], (GROUPS, ROWS), 0, 2) < 1).astype(jnp.int32), jax.random.fold_in(keys[6], 1), 0, 1)
    block_pattern = touch_ends((jax.random.randint(keys[7], (NBLK, NBLK), 0, 4) < 3).astype(jnp.int32), jax.random.fold_in(keys[7], 1), 0, 1)
    return {"row_embed": row_embed, "cotangent": cotangent, "w_qkv": w_qkv, "w_out": w_out, "treat_vec": treat_vec, "is_train": is_train, "treated": treated, "block_pattern": block_pattern}


def allowed_keys(train_row, pattern, row_count):
    expanded = jnp.repeat(jnp.repeat(pattern, BLK, axis=0), BLK, axis=1)
    index_row = jnp.arange(row_count)
    diagonal = index_row[:, None] == index_row[None, :]
    return (expanded == 1) & (train_row[None, :] == 1) | diagonal

def reference(row_embed, cotangent, w_qkv, w_out, treat_vec, is_train, treated, block_pattern):
    scale = 1.0 / math.sqrt(HD)
    wqkv_full = w_qkv.astype(jnp.float32)
    wout_full = w_out.astype(jnp.float32)

    def one_group(items):
        embed, grad_out, train_row, treat_row = items
        shifted = (embed.astype(jnp.float32) + treat_row.astype(jnp.float32)[:, None, None] * treat_vec).astype(jnp.bfloat16)
        shift_full = shifted.astype(jnp.float32)
        projected = jnp.einsum('rfd,ed->rfe', shift_full, wqkv_full).astype(jnp.bfloat16)
        proj_full = projected.astype(jnp.float32)
        query_heads = proj_full[..., :D].reshape(ROWS, FEATS, HEADS, HD)
        key_heads = proj_full[..., D:2 * D].reshape(ROWS, FEATS, HEADS, HD)
        value_heads = proj_full[..., 2 * D:].reshape(ROWS, FEATS, HEADS, HD)
        allowed = allowed_keys(train_row, block_pattern, ROWS)
        scores = jnp.einsum('rfhc,sfhc->fhrs', query_heads, key_heads) * scale
        scores = jnp.where(allowed, scores, -jnp.inf)
        row_peak = lax.optimization_barrier(jnp.max(scores, axis=-1, keepdims=True))
        exp_scores = jnp.exp(scores - row_peak)
        attn_prob = exp_scores / lax.optimization_barrier(jnp.sum(exp_scores, axis=-1, keepdims=True))
        prob_b = attn_prob.astype(jnp.bfloat16)
        prob_full = prob_b.astype(jnp.float32)
        attended = jnp.einsum('fhrs,sfhc->rfhc', prob_full, value_heads).astype(jnp.bfloat16).reshape(ROWS, FEATS, D)
        attn_full = attended.astype(jnp.float32)
        output = (shift_full + jnp.einsum('rfd,ed->rfe', attn_full, wout_full)).astype(jnp.bfloat16)
        grad_full = grad_out.astype(jnp.float32)
        grad_attended = jnp.einsum('rfe,ed->rfd', grad_full, wout_full).astype(jnp.bfloat16)
        grad_att_full = grad_attended.astype(jnp.float32).reshape(ROWS, FEATS, HEADS, HD)
        grad_prob = jnp.einsum('rfhc,sfhc->fhrs', grad_att_full, value_heads)
        row_delta = lax.optimization_barrier(jnp.sum(attn_prob * grad_prob, axis=-1, keepdims=True))
        grad_score = (attn_prob * (grad_prob - row_delta) * scale).astype(jnp.bfloat16).astype(jnp.float32)
        grad_query = jnp.einsum('fhrs,sfhc->rfhc', grad_score, key_heads).astype(jnp.bfloat16)
        grad_key = jnp.einsum('fhrs,rfhc->sfhc', grad_score, query_heads).astype(jnp.bfloat16)
        grad_value = jnp.einsum('fhrs,rfhc->sfhc', prob_full, grad_att_full).astype(jnp.bfloat16)
        grad_projected = jnp.concatenate([grad_query.reshape(ROWS, FEATS, D), grad_key.reshape(ROWS, FEATS, D), grad_value.reshape(ROWS, FEATS, D)], axis=-1)
        gproj_full = grad_projected.astype(jnp.float32)
        grad_in = (grad_full + jnp.einsum('rfe,ed->rfd', gproj_full, wqkv_full)).astype(jnp.bfloat16)
        term_qkv = jnp.einsum('rfe,rfd->ed', gproj_full, shift_full)
        term_out = jnp.einsum('rfe,rfd->ed', grad_full, attn_full)
        return (output, grad_in, term_qkv, term_out)
    output, grad_in, term_qkv, term_out = lax.map(one_group, (row_embed, cotangent, is_train, treated))
    gscale = 1.0 / math.sqrt(GROUPS * ROWS * FEATS)
    weight_grads = jnp.concatenate([lax.optimization_barrier(jnp.sum(term_qkv, axis=0)), lax.optimization_barrier(jnp.sum(term_out, axis=0))], axis=0) * gscale
    return (output, grad_in, weight_grads)
```

```python
import functools
import math

import jax
import jax.numpy as jnp
import numpy as np
from jax import lax
from jax.experimental import pallas as pl
from jax.experimental.pallas import tpu as pltpu
from jax.sharding import Mesh, PartitionSpec as P

HEADS = 8
BLK = 32
F32 = jnp.float32
BF16 = jnp.bfloat16
AXES = ("z_lo", "core", "x", "z_hi", "y")
GRP = ("z_lo", "core")
CELL = ("x", "z_hi", "y")
DEPTH = ("z_hi", "z_lo", "core")
LANES = 128
VMEM = pl.BlockSpec(memory_space=pltpu.VMEM)
SMEM = pl.BlockSpec(memory_space=pltpu.SMEM)


def call(body, out_shape, n_in, scratch=(), smem=(), name=None):
    multi = isinstance(out_shape, (tuple, list))
    return pl.pallas_call(
        body,
        out_shape=out_shape,
        in_specs=[SMEM if i in smem else VMEM for i in range(n_in)],
        out_specs=[VMEM] * len(out_shape) if multi else VMEM,
        scratch_shapes=list(scratch),
        name=name,
    )


def nt(a, b):
    return lax.dot_general(a, b, (((1,), (1,)), ((), ())), preferred_element_type=F32)


def nn(a, b):
    return jnp.dot(a, b, preferred_element_type=F32)


def put_chunks(scr, value, tensor):
    for r in range(2):
        for k in range(4):
            scr[pl.ds(tensor * 8 + r * 4 + k, 64, stride=16), :] = value[
                r * 64 : (r + 1) * 64, k * LANES : (k + 1) * LANES
            ]


def get_chunks(scr, tensor):
    return jnp.concatenate(
        [
            jnp.concatenate(
                [scr[pl.ds(tensor * 8 + r * 4 + k, 64, stride=16), :] for k in range(4)], axis=1
            )
            for r in range(2)
        ],
        axis=0,
    )


def pack_body(treat_rows, embed, cot, treat_vec, send, scr):
    first = lax.axis_index(CELL) * 2
    vec = treat_vec[...]
    shifted = jnp.concatenate(
        [
            embed[0, r].astype(F32) + treat_rows[0, first + r].astype(F32) * vec
            for r in range(2)
        ],
        axis=0,
    )
    put_chunks(scr, shifted, 0)
    put_chunks(scr, jnp.concatenate([cot[0, 0], cot[0, 1]], axis=0).astype(F32), 1)
    send[...] = scr[...].astype(BF16).reshape(64, 16, LANES)


def unpack_body(recv, out, grad_in, scr):
    scr[...] = recv[...].reshape(1024, LANES).astype(F32)
    for tensor, ref in ((0, out), (1, grad_in)):
        value = get_chunks(scr, tensor).astype(BF16)
        ref[0, 0] = value[:64]
        ref[0, 1] = value[64:]


def main_body(recv, w_qkv, w_out, bias, send, keep, rows_out, scr):
    width = w_out.shape[0]
    scale = 1.0 / math.sqrt(width // HEADS)
    scr[...] = recv[...].reshape(1024, LANES).astype(F32)
    shift = get_chunks(scr, 0)
    cot = get_chunks(scr, 1)
    shift_b = shift.astype(BF16)
    cot_b = cot.astype(BF16)
    wq = w_qkv[...]
    wo = w_out[...]
    projected = nt(shift_b, wq).astype(BF16)
    grad_att = nn(cot_b, wo).astype(BF16)
    first = lax.broadcasted_iota(jnp.int32, (128, LANES), 1) < LANES // 2
    zero = jnp.zeros((128, LANES), BF16)
    bias_one = bias[...]
    bias2 = jnp.concatenate([bias_one, bias_one], axis=1)

    def two_heads(slab):
        return jnp.concatenate([jnp.where(first, slab, zero), jnp.where(first, zero, slab)], axis=0)

    def flip(pair):
        return jnp.concatenate([pair[:, :LANES].T, pair[:, LANES:].T], axis=1)

    att, gq, gk, gv = [], [], [], []
    for p in range(width // LANES):
        lo = p * LANES
        q = projected[:, lo : lo + LANES]
        k = projected[:, width + lo : width + lo + LANES]
        v = projected[:, 2 * width + lo : 2 * width + lo + LANES]
        ga = grad_att[:, lo : lo + LANES]
        q2, k2, v2, ga2 = two_heads(q), two_heads(k), two_heads(v), two_heads(ga)
        score = nt(k, q2) + bias2
        grad_prob = nt(v, ga2)
        peak = jnp.max(score, axis=0, keepdims=True)
        exp_score = jnp.exp((score - peak) * scale)
        total = jnp.sum(exp_score, axis=0, keepdims=True)
        prob = exp_score * (1.0 / total)
        prob_b = prob.astype(BF16)
        delta = jnp.sum(prob * grad_prob, axis=0, keepdims=True)
        grad_score = (prob * (grad_prob - delta) * scale).astype(BF16)
        att.append(nn(flip(prob_b), v2).astype(BF16))
        gq.append(nn(flip(grad_score), k2).astype(BF16))
        gk.append(nn(grad_score, q2).astype(BF16))
        gv.append(nn(prob_b, ga2).astype(BF16))
    attended = jnp.concatenate(att, axis=1)
    grad_proj = gq + gk + gv

    mine = lax.axis_index("core") == 0
    tall = [part.T for part in grad_proj] + [
        cot_b[:, k * LANES : (k + 1) * LANES].T for k in range(width // LANES)
    ]
    for n, part in enumerate(tall):
        part = part.reshape(4, 2, 16, LANES)
        even = part[:, 0].reshape(64, LANES)
        odd = part[:, 1].reshape(64, LANES)
        keep[n * 64 : (n + 1) * 64, :] = jnp.where(mine, even, odd)
        send[n * 64 : (n + 1) * 64, :] = jnp.where(mine, odd, even)
    for k in range(width // LANES):
        send[1024 + k * 128 : 1024 + (k + 1) * 128, :] = shift_b[:, k * LANES : (k + 1) * LANES]
        send[1536 + k * 128 : 1536 + (k + 1) * 128, :] = att[k]

    put_chunks(scr, shift + nt(attended, wo), 0)
    put_chunks(scr, cot + nn(jnp.concatenate(grad_proj, axis=1), wq), 1)
    rows_out[...] = scr[...].astype(BF16).reshape(64, 16, LANES)


def weight_body(keep, own, other, partial):
    def tokens(base):
        return jnp.concatenate(
            [
                jnp.concatenate(
                    [ref[base + k * 128 : base + (k + 1) * 128, :] for k in range(4)], axis=1
                )
                for ref in (own, other)
            ],
            axis=0,
        )

    left = jnp.concatenate([keep[...], other[:1024, :]], axis=1)
    shift = tokens(1024)
    att = tokens(1536)
    for x in range(4):
        right = shift if x < 3 else att
        partial[x] = nn(left[x * 256 : (x + 1) * 256], right).astype(BF16)


def sum_x_body(parts, out):
    total = parts[0].astype(F32)
    for x in range(1, 4):
        total = total + parts[x].astype(F32)
    total = total.astype(BF16)
    for z in range(2):
        for y in range(8):
            out[y, z * 16 : (z + 1) * 16, :] = total[(z * 8 + y) * 16 : (z * 8 + y + 1) * 16]


def sum_y_body(parts, out):
    total = parts[0].astype(F32)
    for y in range(1, 8):
        total = total + parts[y].astype(F32)
    total = total.astype(BF16)
    for n in range(16):
        out[n] = total[:16] if n < 8 else total[16:]


def sum_z_body(gscale, parts, out):
    for core in range(2):
        total = parts[core].astype(F32)
        for z in range(1, 8):
            total = total + parts[2 * z + core].astype(F32)
        out[core * 16 : (core + 1) * 16, :] = total * gscale


def key_bias(is_train, pattern):
    train = jnp.transpose(is_train.reshape(64, 2)).reshape(128)
    block = np.tile(np.arange(64) // 16, 2)
    picked = (block[:, None] == np.arange(4)[None, :]).astype(np.float32)
    spread = jnp.einsum("jb,ab,ia->ji", picked, (pattern == 1).astype(F32), picked)
    allowed = ((spread > 0.5) & (train[:, None] == 1)) | np.eye(128, dtype=bool)
    return jnp.where(allowed, 0.0, -jnp.inf).astype(F32)


def per_device(row_embed, cotangent, w_qkv, w_out, treat_vec, is_train, treated, block_pattern):
    chunk = jax.ShapeDtypeStruct((64, 16, LANES), BF16)
    scr = pltpu.VMEM((1024, LANES), F32)
    rows = row_embed.shape
    packed = call(pack_body, chunk, 4, [scr], (0,), "pack")(
        treated, row_embed, cotangent, treat_vec.reshape(1, -1)
    )
    bias = key_bias(is_train[0], block_pattern)
    recv = lax.all_to_all(packed, CELL, 0, 0, tiled=True)
    send, keep, rows_out = call(
        main_body,
        [
            jax.ShapeDtypeStruct((2048, LANES), BF16),
            jax.ShapeDtypeStruct((1024, LANES), BF16),
            chunk,
        ],
        4,
        [scr],
        (),
        "attend",
    )(recv, w_qkv, w_out, bias)
    other = lax.ppermute(send, "core", [(0, 1), (1, 0)])
    partial = call(
        weight_body, jax.ShapeDtypeStruct((4, 256, 512), BF16), 3, name="weight"
    )(keep, send, other)
    by_x = lax.all_to_all(partial, "x", 0, 0, tiled=True)
    part_y = call(sum_x_body, jax.ShapeDtypeStruct((8, 32, 512), BF16), 1, name="sum_x")(by_x)
    by_y = lax.all_to_all(part_y, "y", 0, 0, tiled=True)
    part_z = call(sum_y_body, jax.ShapeDtypeStruct((16, 16, 512), BF16), 1, name="sum_y")(by_y)
    by_z = lax.all_to_all(part_z, DEPTH, 0, 0, tiled=True)
    gscale = 1.0 / math.sqrt(8 * 128 * 64)
    summed = call(
        functools.partial(sum_z_body, gscale),
        jax.ShapeDtypeStruct((32, 512), F32),
        1,
        name="sum_z",
    )(by_z)
    back = lax.all_to_all(rows_out, CELL, 0, 0, tiled=True)
    out, grad_in = call(
        unpack_body,
        [jax.ShapeDtypeStruct(rows, BF16), jax.ShapeDtypeStruct(rows, BF16)],
        1,
        [scr],
        name="unpack",
    )(back)
    return out, grad_in, summed


def solution(mesh):
    fine = Mesh(mesh.devices.reshape(4, 2, 4, 2, 8), AXES)
    cells = P(GRP, CELL, None, None)
    return jax.shard_map(
        per_device,
        mesh=fine,
        in_specs=(cells, cells, P(), P(), P(), P(GRP, None), P(GRP, None), P()),
        out_specs=(cells, cells, P(CELL, None)),
        check_vma=False,
    )
```

```python
import functools
import math

import jax
import jax.numpy as jnp
from jax import lax
from jax.experimental import pallas as pl
from jax.experimental.pallas import tpu as pltpu
from jax.sharding import Mesh, PartitionSpec as P

HEADS = 8
BLK = 32
F32 = jnp.float32
BF16 = jnp.bfloat16
AXES = ("z_lo", "core", "x", "z_hi", "y")
GRP = ("z_lo", "core")
CELL = ("x", "z_hi", "y")
DEPTH = ("z_hi", "z_lo", "core")
LANES = 128
VMEM = pl.BlockSpec(memory_space=pltpu.VMEM)
SMEM = pl.BlockSpec(memory_space=pltpu.SMEM)


def call(body, outs, n_in, scratch=(), smem=(), free=(), name=None):
    run = pl.pallas_call(
        body,
        out_shape=[shape if keep_out else pltpu.VMEM(shape.shape, shape.dtype) for shape, keep_out in outs],
        in_specs=[SMEM if i in smem else VMEM for i in range(n_in)],
        out_specs=[VMEM] * len(outs),
        scratch_shapes=list(scratch),
        name=name,
    )

    def apply(*args):
        return run(
            *[
                a if i in smem or i in free else pltpu.with_memory_space_constraint(a, pltpu.VMEM)
                for i, a in enumerate(args)
            ]
        )

    return apply


def held(*shape, dtype=BF16):
    return (jax.ShapeDtypeStruct(shape, dtype), False)


def given(shape, dtype):
    return (jax.ShapeDtypeStruct(shape, dtype), True)


def nt(a, b):
    return lax.dot_general(a, b, (((1,), (1,)), ((), ())), preferred_element_type=F32)


def nn(a, b):
    return jnp.dot(a, b, preferred_element_type=F32)


def put_chunks(scr, value, tensor):
    for r in range(2):
        for k in range(4):
            scr[pl.ds(tensor * 8 + r * 4 + k, 64, stride=16), :] = value[
                r * 64 : (r + 1) * 64, k * LANES : (k + 1) * LANES
            ]


def get_chunks(scr, tensor):
    return jnp.concatenate(
        [
            jnp.concatenate(
                [scr[pl.ds(tensor * 8 + r * 4 + k, 64, stride=16), :] for k in range(4)], axis=1
            )
            for r in range(2)
        ],
        axis=0,
    )


def pack_body(treat_rows, embed, cot, treat_vec, send, scr):
    first = lax.axis_index(CELL) * 2
    vec = treat_vec[...]
    shifted = jnp.concatenate(
        [
            embed[0, r].astype(F32) + treat_rows[0, first + r].astype(F32) * vec
            for r in range(2)
        ],
        axis=0,
    )
    put_chunks(scr, shifted, 0)
    put_chunks(scr, jnp.concatenate([cot[0, 0], cot[0, 1]], axis=0).astype(F32), 1)
    send[...] = scr[...].astype(BF16).reshape(64, 16, LANES)


def unpack_body(recv, out, grad_in, scr):
    scr[...] = recv[...].reshape(1024, LANES).astype(F32)
    for tensor, ref in ((0, out), (1, grad_in)):
        value = get_chunks(scr, tensor).astype(BF16)
        ref[0, 0] = value[:64]
        ref[0, 1] = value[64:]


def main_body(recv, w_qkv, w_out, bias, send, keep, rows_out, scr):
    width = w_out.shape[0]
    scale = 1.0 / math.sqrt(width // HEADS)
    scr[...] = recv[...].reshape(1024, LANES).astype(F32)
    shift = get_chunks(scr, 0)
    cot = get_chunks(scr, 1)
    shift_b = shift.astype(BF16)
    cot_b = cot.astype(BF16)
    wq = w_qkv[...]
    wo = w_out[...]
    projected = nt(shift_b, wq).astype(BF16)
    grad_att = nn(cot_b, wo).astype(BF16)
    first = lax.broadcasted_iota(jnp.int32, (128, LANES), 1) < LANES // 2
    zero = jnp.zeros((128, LANES), BF16)
    bias_one = bias[...]
    bias2 = jnp.concatenate([bias_one, bias_one], axis=1)

    def two_heads(slab):
        return jnp.concatenate([jnp.where(first, slab, zero), jnp.where(first, zero, slab)], axis=0)

    def flip(pair):
        return jnp.concatenate([pair[:, :LANES].T, pair[:, LANES:].T], axis=1)

    att, gq, gk, gv = [], [], [], []
    for p in range(width // LANES):
        lo = p * LANES
        q = projected[:, lo : lo + LANES]
        k = projected[:, width + lo : width + lo + LANES]
        v = projected[:, 2 * width + lo : 2 * width + lo + LANES]
        ga = grad_att[:, lo : lo + LANES]
        q2, k2, v2, ga2 = two_heads(q), two_heads(k), two_heads(v), two_heads(ga)
        score = nt(k, q2) + bias2
        grad_prob = nt(v, ga2)
        peak = jnp.max(score, axis=0, keepdims=True)
        exp_score = jnp.exp((score - peak) * scale)
        total = jnp.sum(exp_score, axis=0, keepdims=True)
        prob = exp_score * (1.0 / total)
        prob_b = prob.astype(BF16)
        delta = jnp.sum(prob * grad_prob, axis=0, keepdims=True)
        grad_score = (prob * (grad_prob - delta) * scale).astype(BF16)
        att.append(nn(flip(prob_b), v2).astype(BF16))
        gq.append(nn(flip(grad_score), k2).astype(BF16))
        gk.append(nn(grad_score, q2).astype(BF16))
        gv.append(nn(prob_b, ga2).astype(BF16))
    attended = jnp.concatenate(att, axis=1)
    grad_proj = gq + gk + gv

    mine = lax.axis_index("core") == 0
    tall = [part.T for part in grad_proj] + [
        cot_b[:, k * LANES : (k + 1) * LANES].T for k in range(width // LANES)
    ]
    for n, part in enumerate(tall):
        part = part.reshape(4, 2, 16, LANES)
        even = part[:, 0].reshape(64, LANES)
        odd = part[:, 1].reshape(64, LANES)
        keep[n * 64 : (n + 1) * 64, :] = jnp.where(mine, even, odd)
        send[n * 64 : (n + 1) * 64, :] = jnp.where(mine, odd, even)
    for k in range(width // LANES):
        send[1024 + k * 128 : 1024 + (k + 1) * 128, :] = shift_b[:, k * LANES : (k + 1) * LANES]
        send[1536 + k * 128 : 1536 + (k + 1) * 128, :] = att[k]

    put_chunks(scr, shift + nt(attended, wo), 0)
    put_chunks(scr, cot + nn(jnp.concatenate(grad_proj, axis=1), wq), 1)
    rows_out[...] = scr[...].astype(BF16).reshape(64, 16, LANES)


def weight_body(keep, own, other, *chunks):
    def tokens(base):
        return jnp.concatenate(
            [
                jnp.concatenate(
                    [ref[base + k * 128 : base + (k + 1) * 128, :] for k in range(4)], axis=1
                )
                for ref in (own, other)
            ],
            axis=0,
        )

    shift = tokens(1024)
    att = tokens(1536)
    x = lax.axis_index("x")
    for d, chunk in enumerate(chunks):
        place = lax.rem(x + d, 4)
        here = pl.ds(pl.multiple_of(place * 256, 256), 256)
        left = jnp.concatenate([keep[here, :], other[here, :]], axis=1)
        right = jnp.where(place == 3, att, shift)
        chunk[...] = nn(left, right).astype(BF16)


def sum_x_body(own, a, b, c, after, out):
    total = own[...].astype(F32)
    for part in (a, b, c):
        total = total + part[...].astype(F32)
    total = total.astype(BF16)
    for z in range(2):
        for y in range(8):
            out[y, z * 16 : (z + 1) * 16, :] = total[(z * 8 + y) * 16 : (z * 8 + y + 1) * 16]


def sum_y_body(parts, out):
    total = parts[0].astype(F32)
    for y in range(1, 8):
        total = total + parts[y].astype(F32)
    total = total.astype(BF16)
    for n in range(16):
        out[n] = total[:16] if n < 8 else total[16:]


def sum_z_body(gscale, parts, out):
    for core in range(2):
        total = parts[core].astype(F32)
        for z in range(1, 8):
            total = total + parts[2 * z + core].astype(F32)
        out[core * 16 : (core + 1) * 16, :] = total * gscale


def prep_body(pattern, train, w_qkv, w_out, bias, w_qkv_here, w_out_here):
    key = lax.broadcasted_iota(jnp.int32, (128, 128), 0)
    query = lax.broadcasted_iota(jnp.int32, (128, 128), 1)
    key_block = lax.rem(key, 64) // 16
    query_block = lax.rem(query, 64) // 16
    open_block = jnp.zeros((128, 128), jnp.int32)
    for a in range(4):
        for b in range(4):
            here = (query_block == a) & (key_block == b)
            open_block = jnp.where(here, pattern[a, b], open_block)
    allowed = ((open_block == 1) & (train[...] == 1)) | (key == query)
    bias[...] = jnp.where(allowed, 0.0, -jnp.inf).astype(F32)
    w_qkv_here[...] = w_qkv[...]
    w_out_here[...] = w_out[...]


def per_device(row_embed, cotangent, w_qkv, w_out, treat_vec, is_train, treated, block_pattern):
    scr = pltpu.VMEM((1024, LANES), F32)
    rows = row_embed.shape
    (packed,) = call(pack_body, [held(64, 16, LANES)], 4, [scr], (0,), (1, 2, 3), "pack")(
        treated, row_embed, cotangent, treat_vec.reshape(1, -1)
    )
    train = jnp.transpose(is_train.reshape(64, 2)).reshape(128, 1)
    bias, w_qkv, w_out = call(
        prep_body,
        [held(128, 128, dtype=F32), held(*w_qkv.shape), held(*w_out.shape)],
        4,
        smem=(0,),
        free=(1, 2, 3),
        name="prep",
    )(block_pattern, train, w_qkv, w_out)
    recv = lax.all_to_all(packed, CELL, 0, 0, tiled=True)
    send, keep, rows_out = call(
        main_body,
        [held(2048, LANES), held(1024, LANES), held(64, 16, LANES)],
        4,
        [scr],
        name="attend",
    )(recv, w_qkv, w_out, bias)
    other = lax.ppermute(send, "core", [(0, 1), (1, 0)])
    chunks = call(weight_body, [held(256, 512)] * 4, 3, name="weight")(keep, send, other)
    by_x = [chunks[0]] + [
        lax.ppermute(chunks[d], "x", [(i, (i + d) % 4) for i in range(4)]) for d in (2, 1, 3)
    ]
    back = lax.all_to_all(rows_out, CELL, 0, 0, tiled=True)
    (part_y,) = call(sum_x_body, [held(8, 32, 512)], 5, name="sum_x")(*by_x, back)
    by_y = lax.all_to_all(part_y, "y", 0, 0, tiled=True)
    (part_z,) = call(sum_y_body, [held(16, 16, 512)], 1, name="sum_y")(by_y)
    by_z = lax.all_to_all(part_z, DEPTH, 0, 0, tiled=True)
    gscale = 1.0 / math.sqrt(8 * 128 * 64)
    (summed,) = call(
        functools.partial(sum_z_body, gscale), [given((32, 512), F32)], 1, name="sum_z"
    )(by_z)
    out, grad_in = call(
        unpack_body, [given(rows, BF16), given(rows, BF16)], 1, [scr], name="unpack"
    )(back)
    return out, grad_in, summed


def solution(mesh):
    fine = Mesh(mesh.devices.reshape(4, 2, 4, 2, 8), AXES)
    cells = P(GRP, CELL, None, None)
    return jax.shard_map(
        per_device,
        mesh=fine,
        in_specs=(cells, cells, P(), P(), P(), P(GRP, None), P(GRP, None), P()),
        out_specs=(cells, cells, P(CELL, None)),
        check_vma=False,
    )
```

```python
import functools
import math

import jax
import jax.numpy as jnp
from jax import lax
from jax.experimental import pallas as pl
from jax.experimental.pallas import tpu as pltpu
from jax.sharding import Mesh, PartitionSpec as P

HEADS = 8
BLK = 32
F32 = jnp.float32
BF16 = jnp.bfloat16
AXES = ("z_lo", "core", "x", "z_hi", "y")
GRP = ("z_lo", "core")
CELL = ("x", "z_hi", "y")
ROWS = ("z_hi", "y")
LANES = 128
VMEM = pl.BlockSpec(memory_space=pltpu.VMEM)
SMEM = pl.BlockSpec(memory_space=pltpu.SMEM)


def call(body, outs, n_in, scratch=(), smem=(), free=(), name=None):
    run = pl.pallas_call(
        body,
        out_shape=[shape if keep_out else pltpu.VMEM(shape.shape, shape.dtype) for shape, keep_out in outs],
        in_specs=[SMEM if i in smem else VMEM for i in range(n_in)],
        out_specs=[VMEM] * len(outs),
        scratch_shapes=list(scratch),
        compiler_params=None if free else pltpu.CompilerParams(vmem_limit_bytes=16 * 2**20),
        name=name,
    )

    def apply(*args):
        return run(
            *[
                a if i in smem or i in free else pltpu.with_memory_space_constraint(a, pltpu.VMEM)
                for i, a in enumerate(args)
            ]
        )

    return apply


def held(*shape, dtype=BF16):
    return (jax.ShapeDtypeStruct(shape, dtype), False)


def given(shape, dtype):
    return (jax.ShapeDtypeStruct(shape, dtype), True)


def nt(a, b):
    return lax.dot_general(a, b, (((1,), (1,)), ((), ())), preferred_element_type=F32)


def nn(a, b):
    return jnp.dot(a, b, preferred_element_type=F32)


def put_chunks(scr, value, tensor):
    for r in range(2):
        for k in range(4):
            scr[pl.ds(tensor * 8 + r * 4 + k, 64, stride=16), :] = value[
                r * 64 : (r + 1) * 64, k * LANES : (k + 1) * LANES
            ]


def get_chunks(scr, tensor):
    return jnp.concatenate(
        [
            jnp.concatenate(
                [scr[pl.ds(tensor * 8 + r * 4 + k, 64, stride=16), :] for k in range(4)], axis=1
            )
            for r in range(2)
        ],
        axis=0,
    )


def pack_body(treat_rows, embed, cot, treat_vec, send, scr):
    first = lax.axis_index(CELL) * 2
    vec = treat_vec[...]
    shifted = jnp.concatenate(
        [
            embed[0, r].astype(F32) + treat_rows[0, first + r].astype(F32) * vec
            for r in range(2)
        ],
        axis=0,
    )
    put_chunks(scr, shifted, 0)
    put_chunks(scr, jnp.concatenate([cot[0, 0], cot[0, 1]], axis=0).astype(F32), 1)
    send[...] = scr[...].astype(BF16).reshape(64, 16, LANES)


def unpack_body(recv, out, grad_in, *scr):
    for k, part in enumerate(scr):
        lanes = slice(k * LANES, (k + 1) * LANES)
        part[...] = recv[:, 16:, lanes].astype(F32).reshape(256, LANES)
        for x in range(4):
            for n, ref in enumerate((out, grad_in)):
                for r in range(2):
                    ref[0, r, x * 16 : (x + 1) * 16, lanes] = part[
                        pl.ds(x * 4 + 2 * n + r, 16, stride=16), :
                    ].astype(BF16)


def main_body(recv, w_qkv, w_out, bias, send, keep, rows_out, scr):
    width = w_out.shape[0]
    scale = 1.0 / math.sqrt(width // HEADS)
    scr[...] = recv[...].reshape(1024, LANES).astype(F32)
    shift = get_chunks(scr, 0)
    cot = get_chunks(scr, 1)
    shift_b = shift.astype(BF16)
    cot_b = cot.astype(BF16)
    wq = w_qkv[...]
    wo = w_out[...]
    projected = nt(shift_b, wq).astype(BF16)
    grad_att = nn(cot_b, wo).astype(BF16)
    first = lax.broadcasted_iota(jnp.int32, (128, LANES), 1) < LANES // 2
    zero = jnp.zeros((128, LANES), BF16)
    bias_one = bias[...]
    bias2 = jnp.concatenate([bias_one, bias_one], axis=1)

    def two_heads(slab):
        return jnp.concatenate([jnp.where(first, slab, zero), jnp.where(first, zero, slab)], axis=0)

    def flip(pair):
        return jnp.concatenate([pair[:, :LANES].T, pair[:, LANES:].T], axis=1)

    att, gq, gk, gv = [], [], [], []
    for p in range(width // LANES):
        lo = p * LANES
        q = projected[:, lo : lo + LANES]
        k = projected[:, width + lo : width + lo + LANES]
        v = projected[:, 2 * width + lo : 2 * width + lo + LANES]
        ga = grad_att[:, lo : lo + LANES]
        q2, k2, v2, ga2 = two_heads(q), two_heads(k), two_heads(v), two_heads(ga)
        score = nt(k, q2) + bias2
        grad_prob = nt(v, ga2)
        peak = jnp.max(score, axis=0, keepdims=True)
        exp_score = jnp.exp((score - peak) * scale)
        total = jnp.sum(exp_score, axis=0, keepdims=True)
        prob = exp_score * (1.0 / total)
        prob_b = prob.astype(BF16)
        delta = jnp.sum(prob * grad_prob, axis=0, keepdims=True)
        grad_score = (prob * (grad_prob - delta) * scale).astype(BF16)
        att.append(nn(flip(prob_b), v2).astype(BF16))
        gq.append(nn(flip(grad_score), k2).astype(BF16))
        gk.append(nn(grad_score, q2).astype(BF16))
        gv.append(nn(prob_b, ga2).astype(BF16))
    attended = jnp.concatenate(att, axis=1)
    grad_proj = gq + gk + gv

    mine = lax.axis_index("core") == 0
    tall = [part.T for part in grad_proj] + [
        cot_b[:, k * LANES : (k + 1) * LANES].T for k in range(width // LANES)
    ]
    for n, part in enumerate(tall):
        part = part.reshape(4, 2, 16, LANES)
        even = part[:, 0].reshape(64, LANES)
        odd = part[:, 1].reshape(64, LANES)
        keep[n * 64 : (n + 1) * 64, :] = jnp.where(mine, even, odd)
        send[n * 64 : (n + 1) * 64, :] = jnp.where(mine, odd, even)
    for k in range(width // LANES):
        send[1024 + k * 128 : 1024 + (k + 1) * 128, :] = shift_b[:, k * LANES : (k + 1) * LANES]
        send[1536 + k * 128 : 1536 + (k + 1) * 128, :] = att[k]

    out = (shift + nt(attended, wo)).astype(BF16)
    grad_in = (cot + nn(jnp.concatenate(grad_proj, axis=1), wq)).astype(BF16)
    for x in range(4):
        for n, value in enumerate((out, grad_in)):
            for r in range(2):
                rows_out[x, (2 * n + r) * 16 : (2 * n + r + 1) * 16, :] = value[
                    r * 64 + x * 16 : r * 64 + (x + 1) * 16
                ]


def weight_body(keep, own, other, rows_out, merged):
    def tokens(base):
        return jnp.concatenate(
            [
                jnp.concatenate(
                    [ref[base + k * 128 : base + (k + 1) * 128, :] for k in range(4)], axis=1
                )
                for ref in (own, other)
            ],
            axis=0,
        )

    left = jnp.concatenate([keep[...], other[:1024, :]], axis=1)
    shift = tokens(1024)
    att = tokens(1536)
    for x in range(4):
        right = shift if x < 3 else att
        merged[x, :256, :] = nn(left[x * 256 : (x + 1) * 256], right).astype(BF16)
        merged[x, 256:, :] = rows_out[x]


def sum_x_body(parts, out, *scr):
    total = parts[0, :256].astype(F32)
    for x in range(1, 4):
        total = total + parts[x, :256].astype(F32)
    out[:, :16, :] = total.astype(BF16).reshape(16, 16, 512)
    for k, part in enumerate(scr):
        lanes = slice(k * LANES, (k + 1) * LANES)
        for x in range(4):
            for m in range(4):
                part[pl.ds(x * 4 + m, 16, stride=16), :] = parts[
                    x, 256 + m * 16 : 256 + (m + 1) * 16, lanes
                ].astype(F32)
        out[:, 16:, lanes] = part[...].astype(BF16).reshape(16, 16, LANES)


def sum_rows_body(parts, out):
    total = parts[0, :16].astype(F32)
    for n in range(1, 16):
        total = total + parts[n, :16].astype(F32)
    total = total.astype(BF16)
    for n in range(8):
        out[n] = total


def sum_z_body(gscale, parts, out):
    for core in range(2):
        total = parts[core].astype(F32)
        for z in range(1, 4):
            total = total + parts[2 * z + core].astype(F32)
        out[core * 16 : (core + 1) * 16, :] = total * gscale


def prep_body(pattern, train, w_qkv, w_out, bias, w_qkv_here, w_out_here):
    key = lax.broadcasted_iota(jnp.int32, (128, 128), 0)
    query = lax.broadcasted_iota(jnp.int32, (128, 128), 1)
    key_block = lax.rem(key, 64) // 16
    query_block = lax.rem(query, 64) // 16
    open_block = jnp.zeros((128, 128), jnp.int32)
    for a in range(4):
        for b in range(4):
            here = (query_block == a) & (key_block == b)
            open_block = jnp.where(here, pattern[a, b], open_block)
    allowed = ((open_block == 1) & (train[...] == 1)) | (key == query)
    bias[...] = jnp.where(allowed, 0.0, -jnp.inf).astype(F32)
    w_qkv_here[...] = w_qkv[...]
    w_out_here[...] = w_out[...]


def per_device(row_embed, cotangent, w_qkv, w_out, treat_vec, is_train, treated, block_pattern):
    scr = pltpu.VMEM((1024, LANES), F32)
    rows = row_embed.shape
    (packed,) = call(pack_body, [held(64, 16, LANES)], 4, [scr], (0,), (1, 2, 3), "pack")(
        treated, row_embed, cotangent, treat_vec.reshape(1, -1)
    )
    train = jnp.transpose(is_train.reshape(64, 2)).reshape(128, 1)
    bias, w_qkv, w_out = call(
        prep_body,
        [held(128, 128, dtype=F32), held(*w_qkv.shape), held(*w_out.shape)],
        4,
        smem=(0,),
        free=(1, 2, 3),
        name="prep",
    )(block_pattern, train, w_qkv, w_out)
    recv = lax.all_to_all(packed, CELL, 0, 0, tiled=True)
    send, keep, rows_out = call(
        main_body,
        [held(2048, LANES), held(1024, LANES), held(4, 64, 512)],
        4,
        [scr],
        name="attend",
    )(recv, w_qkv, w_out, bias)
    other = lax.ppermute(send, "core", [(0, 1), (1, 0)])
    (merged,) = call(weight_body, [held(4, 320, 512)], 4, name="weight")(
        keep, send, other, rows_out
    )
    by_x = lax.all_to_all(merged, "x", 0, 0, tiled=True)
    tall = [pltpu.VMEM((256, LANES), F32)] * 4
    (part_rows,) = call(sum_x_body, [held(16, 32, 512)], 1, tall, name="sum_x")(by_x)
    by_rows = lax.all_to_all(part_rows, ROWS, 0, 0, tiled=True)
    (part_z,) = call(sum_rows_body, [held(8, 16, 512)], 1, name="sum_rows")(by_rows)
    by_z = lax.all_to_all(part_z, GRP, 0, 0, tiled=True)
    gscale = 1.0 / math.sqrt(8 * 128 * 64)
    (summed,) = call(
        functools.partial(sum_z_body, gscale), [given((32, 512), F32)], 1, name="sum_z"
    )(by_z)
    out, grad_in = call(
        unpack_body, [given(rows, BF16), given(rows, BF16)], 1, tall, name="unpack"
    )(by_rows)
    return out, grad_in, summed


def solution(mesh):
    fine = Mesh(mesh.devices.reshape(4, 2, 4, 2, 8), AXES)
    cells = P(GRP, CELL, None, None)
    return jax.shard_map(
        per_device,
        mesh=fine,
        in_specs=(cells, cells, P(), P(), P(), P(GRP, None), P(GRP, None), P()),
        out_specs=(cells, cells, P(CELL, None)),
        check_vma=False,
    )
```

```python
import functools
import math

import jax
import jax.numpy as jnp
from jax import lax
from jax.experimental import pallas as pl
from jax.experimental.pallas import tpu as pltpu
from jax.sharding import Mesh, PartitionSpec as P

HEADS = 8
BLK = 32
F32 = jnp.float32
BF16 = jnp.bfloat16
AXES = ("z_lo", "core", "x", "z_hi", "y_hi", "y_lo")
GRP = ("z_lo", "core")
CELL = ("x", "z_hi", "y_hi", "y_lo")
NEAR = ("x", "y_lo")
FAR = ("z_hi", "y_hi")
LANES = 128
VMEM = pl.BlockSpec(memory_space=pltpu.VMEM)
SMEM = pl.BlockSpec(memory_space=pltpu.SMEM)


def call(body, outs, n_in, scratch=(), smem=(), free=(), name=None):
    run = pl.pallas_call(
        body,
        out_shape=[shape if keep_out else pltpu.VMEM(shape.shape, shape.dtype) for shape, keep_out in outs],
        in_specs=[SMEM if i in smem else VMEM for i in range(n_in)],
        out_specs=[VMEM] * len(outs),
        scratch_shapes=list(scratch),
        compiler_params=None if free else pltpu.CompilerParams(vmem_limit_bytes=16 * 2**20),
        name=name,
    )

    def apply(*args):
        return run(
            *[
                a if i in smem or i in free else pltpu.with_memory_space_constraint(a, pltpu.VMEM)
                for i, a in enumerate(args)
            ]
        )

    return apply


def held(*shape, dtype=BF16):
    return (jax.ShapeDtypeStruct(shape, dtype), False)


def given(shape, dtype):
    return (jax.ShapeDtypeStruct(shape, dtype), True)


def nt(a, b):
    return lax.dot_general(a, b, (((1,), (1,)), ((), ())), preferred_element_type=F32)


def nn(a, b):
    return jnp.dot(a, b, preferred_element_type=F32)


def put_chunks(scr, value, tensor):
    for r in range(2):
        for k in range(4):
            scr[pl.ds(tensor * 8 + r * 4 + k, 64, stride=16), :] = value[
                r * 64 : (r + 1) * 64, k * LANES : (k + 1) * LANES
            ]


def get_chunks(scr, tensor):
    return jnp.concatenate(
        [
            jnp.concatenate(
                [scr[pl.ds(tensor * 8 + r * 4 + k, 64, stride=16), :] for k in range(4)], axis=1
            )
            for r in range(2)
        ],
        axis=0,
    )


def pack_body(treat_rows, embed, cot, treat_vec, send, scr):
    first = lax.axis_index(CELL) * 2
    vec = treat_vec[...]
    shifted = jnp.concatenate(
        [
            embed[0, r].astype(F32) + treat_rows[0, first + r].astype(F32) * vec
            for r in range(2)
        ],
        axis=0,
    )
    put_chunks(scr, shifted, 0)
    put_chunks(scr, jnp.concatenate([cot[0, 0], cot[0, 1]], axis=0).astype(F32), 1)
    send[...] = scr[...].astype(BF16).reshape(64, 16, LANES)


def unpack_body(recv, out, grad_in, *scr):
    for k in range(4):
        lanes = slice(k * LANES, (k + 1) * LANES)
        part, flat = scr[k], scr[4 + k]
        part[...] = recv[:, 16:, lanes].astype(F32).reshape(256, LANES)
        for x in range(4):
            for y in range(2):
                for m in range(4):
                    flat[pl.ds(m * 64 + x * 16 + y, 8, stride=2), :] = part[
                        pl.ds((2 * x + y) * 4 + m, 8, stride=32), :
                    ]
        for m in range(4):
            ref = out if m < 2 else grad_in
            ref[0, m % 2, :, lanes] = flat[m * 64 : (m + 1) * 64, :].astype(BF16)


def main_body(recv, w_qkv, w_out, bias, send, keep, grads, scr):
    width = w_out.shape[0]
    scale = 1.0 / math.sqrt(width // HEADS)
    scr[...] = recv[...].reshape(1024, LANES).astype(F32)
    shift = get_chunks(scr, 0)
    cot = get_chunks(scr, 1)
    shift_b = shift.astype(BF16)
    cot_b = cot.astype(BF16)
    wq = w_qkv[...]
    wo = w_out[...]
    projected = nt(shift_b, wq).astype(BF16)
    grad_att = nn(cot_b, wo).astype(BF16)
    first = lax.broadcasted_iota(jnp.int32, (128, LANES), 1) < LANES // 2
    zero = jnp.zeros((128, LANES), BF16)
    bias_one = bias[...]
    bias2 = jnp.concatenate([bias_one, bias_one], axis=1)

    def two_heads(slab):
        return jnp.concatenate([jnp.where(first, slab, zero), jnp.where(first, zero, slab)], axis=0)

    def flip(pair):
        return jnp.concatenate([pair[:, :LANES].T, pair[:, LANES:].T], axis=1)

    att, gq, gk, gv = [], [], [], []
    for p in range(width // LANES):
        lo = p * LANES
        q = projected[:, lo : lo + LANES]
        k = projected[:, width + lo : width + lo + LANES]
        v = projected[:, 2 * width + lo : 2 * width + lo + LANES]
        ga = grad_att[:, lo : lo + LANES]
        q2, k2, v2, ga2 = two_heads(q), two_heads(k), two_heads(v), two_heads(ga)
        score = nt(k, q2) + bias2
        grad_prob = nt(v, ga2)
        peak = jnp.max(score, axis=0, keepdims=True)
        exp_score = jnp.exp((score - peak) * scale)
        total = jnp.sum(exp_score, axis=0, keepdims=True)
        prob = exp_score * (1.0 / total)
        prob_b = prob.astype(BF16)
        delta = jnp.sum(prob * grad_prob, axis=0, keepdims=True)
        grad_score = (prob * (grad_prob - delta) * scale).astype(BF16)
        att.append(nn(flip(prob_b), v2).astype(BF16))
        gq.append(nn(flip(grad_score), k2).astype(BF16))
        gk.append(nn(grad_score, q2).astype(BF16))
        gv.append(nn(prob_b, ga2).astype(BF16))
    grad_proj = gq + gk + gv

    mine = lax.axis_index("core") == 0
    tall = [part.T for part in grad_proj] + [
        cot_b[:, k * LANES : (k + 1) * LANES].T for k in range(width // LANES)
    ]
    for n, part in enumerate(tall):
        part = part.reshape(4, 2, 16, LANES)
        even = part[:, 0].reshape(64, LANES)
        odd = part[:, 1].reshape(64, LANES)
        keep[n * 64 : (n + 1) * 64, :] = jnp.where(mine, even, odd)
        send[n * 64 : (n + 1) * 64, :] = jnp.where(mine, odd, even)
    for k in range(width // LANES):
        send[1024 + k * 128 : 1024 + (k + 1) * 128, :] = shift_b[:, k * LANES : (k + 1) * LANES]
        send[1536 + k * 128 : 1536 + (k + 1) * 128, :] = att[k]

    for p, part in enumerate(grad_proj):
        grads[:, p * LANES : (p + 1) * LANES] = part


def rows_body(recv, own, grads, w_qkv, w_out, rows_out, scr):
    width = w_out.shape[0]
    scr[...] = recv[...].reshape(1024, LANES).astype(F32)
    shift = get_chunks(scr, 0)
    cot = get_chunks(scr, 1)
    attended = jnp.concatenate(
        [own[1536 + k * 128 : 1536 + (k + 1) * 128, :] for k in range(width // LANES)], axis=1
    )
    out = shift + nt(attended, w_out[...])
    grad_in = cot + nn(grads[...], w_qkv[...])
    for k in range(width // LANES):
        lanes = slice(k * LANES, (k + 1) * LANES)
        here = scr.at[k * 256 : (k + 1) * 256]
        here[:128, :] = out[:, lanes]
        here[128:, :] = grad_in[:, lanes]
        for x in range(4):
            for y in range(2):
                for m in range(4):
                    rows_out[2 * x + y, m * 8 : (m + 1) * 8, lanes] = here[
                        pl.ds(m * 64 + x * 16 + y, 8, stride=2), :
                    ].astype(BF16)


def weight_body(keep, own, other, rows_out, merged):
    def tokens(base):
        return jnp.concatenate(
            [
                jnp.concatenate(
                    [ref[base + k * 128 : base + (k + 1) * 128, :] for k in range(4)], axis=1
                )
                for ref in (own, other)
            ],
            axis=0,
        )

    left = jnp.concatenate([keep[...], other[:1024, :]], axis=1)
    shift = tokens(1024)
    att = tokens(1536)
    for x in range(4):
        right = shift if x < 3 else att
        block = nn(left[x * 256 : (x + 1) * 256], right).astype(BF16).reshape(8, 2, 16, 512)
        for y in range(2):
            merged[2 * x + y, :128, :] = block[:, y].reshape(128, 512)
            merged[2 * x + y, 128:, :] = rows_out[2 * x + y]


def sum_near_body(parts, out, *scr):
    total = parts[0, :128].astype(F32)
    for n in range(1, 8):
        total = total + parts[n, :128].astype(F32)
    out[:, :16, :] = total.astype(BF16).reshape(8, 16, 512)
    for k, part in enumerate(scr):
        lanes = slice(k * LANES, (k + 1) * LANES)
        for n in range(8):
            for m in range(4):
                part[pl.ds(n * 4 + m, 8, stride=32), :] = parts[
                    n, 128 + m * 8 : 128 + (m + 1) * 8, lanes
                ].astype(F32)
        out[:, 16:, lanes] = part[...].astype(BF16).reshape(8, 32, LANES)


def sum_far_body(parts, out):
    total = parts[0, :16].astype(F32)
    for n in range(1, 8):
        total = total + parts[n, :16].astype(F32)
    total = total.astype(BF16)
    for n in range(8):
        out[n] = total


def sum_z_body(gscale, parts, out):
    for core in range(2):
        total = parts[core].astype(F32)
        for z in range(1, 4):
            total = total + parts[2 * z + core].astype(F32)
        out[core * 16 : (core + 1) * 16, :] = total * gscale


def prep_body(pattern, train, w_qkv, w_out, bias, w_qkv_here, w_out_here):
    key = lax.broadcasted_iota(jnp.int32, (128, 128), 0)
    query = lax.broadcasted_iota(jnp.int32, (128, 128), 1)
    key_block = lax.rem(key, 64) // 16
    query_block = lax.rem(query, 64) // 16
    open_block = jnp.zeros((128, 128), jnp.int32)
    for a in range(4):
        for b in range(4):
            here = (query_block == a) & (key_block == b)
            open_block = jnp.where(here, pattern[a, b], open_block)
    allowed = ((open_block == 1) & (train[...] == 1)) | (key == query)
    bias[...] = jnp.where(allowed, 0.0, -jnp.inf).astype(F32)
    w_qkv_here[...] = w_qkv[...]
    w_out_here[...] = w_out[...]


def per_device(row_embed, cotangent, w_qkv, w_out, treat_vec, is_train, treated, block_pattern):
    scr = pltpu.VMEM((1024, LANES), F32)
    rows = row_embed.shape
    (packed,) = call(pack_body, [held(64, 16, LANES)], 4, [scr], (0,), (1, 2, 3), "pack")(
        treated, row_embed, cotangent, treat_vec.reshape(1, -1)
    )
    train = jnp.transpose(is_train.reshape(64, 2)).reshape(128, 1)
    bias, w_qkv, w_out = call(
        prep_body,
        [held(128, 128, dtype=F32), held(*w_qkv.shape), held(*w_out.shape)],
        4,
        smem=(0,),
        free=(1, 2, 3),
        name="prep",
    )(block_pattern, train, w_qkv, w_out)
    recv = lax.all_to_all(packed, CELL, 0, 0, tiled=True)
    send, keep, grads = call(
        main_body,
        [held(2048, LANES), held(1024, LANES), held(128, 1536)],
        4,
        [scr],
        name="attend",
    )(recv, w_qkv, w_out, bias)
    other = lax.ppermute(send, "core", [(0, 1), (1, 0)])
    (rows_out,) = call(rows_body, [held(8, 32, 512)], 5, [scr], name="rows")(
        recv, send, grads, w_qkv, w_out
    )
    (merged,) = call(weight_body, [held(8, 160, 512)], 4, name="weight")(
        keep, send, other, rows_out
    )
    by_near = lax.all_to_all(merged, NEAR, 0, 0, tiled=True)
    tall = [pltpu.VMEM((256, LANES), F32)] * 4
    (part_near,) = call(sum_near_body, [held(8, 48, 512)], 1, tall, name="sum_near")(by_near)
    by_far = lax.all_to_all(part_near, FAR, 0, 0, tiled=True)
    (part_far,) = call(sum_far_body, [held(8, 16, 512)], 1, name="sum_far")(by_far)
    by_z = lax.all_to_all(part_far, GRP, 0, 0, tiled=True)
    gscale = 1.0 / math.sqrt(8 * 128 * 64)
    (summed,) = call(
        functools.partial(sum_z_body, gscale), [given((32, 512), F32)], 1, name="sum_z"
    )(by_z)
    out, grad_in = call(
        unpack_body, [given(rows, BF16), given(rows, BF16)], 1, tall * 2, name="unpack"
    )(by_far)
    return out, grad_in, summed


def solution(mesh):
    fine = Mesh(mesh.devices.reshape(4, 2, 4, 2, 4, 2), AXES)
    cells = P(GRP, CELL, None, None)
    return jax.shard_map(
        per_device,
        mesh=fine,
        in_specs=(cells, cells, P(), P(), P(), P(GRP, None), P(GRP, None), P()),
        out_specs=(cells, cells, P(CELL, None)),
        check_vma=False,
    )
```

```python
import functools
import math

import jax
import jax.numpy as jnp
from jax import lax
from jax.experimental import pallas as pl
from jax.experimental.pallas import tpu as pltpu
from jax.sharding import Mesh, PartitionSpec as P

HEADS = 8
BLK = 32
F32 = jnp.float32
BF16 = jnp.bfloat16
AXES = ("z_lo", "core", "x", "z_hi", "y_hi", "y_lo")
GRP = ("z_lo", "core")
CELL = ("x", "z_hi", "y_hi", "y_lo")
NEAR = ("x", "y_lo")
FAR = ("z_hi", "y_hi")
LANES = 128
VMEM = pl.BlockSpec(memory_space=pltpu.VMEM)
SMEM = pl.BlockSpec(memory_space=pltpu.SMEM)


def call(body, outs, n_in, scratch=(), smem=(), free=(), name=None):
    run = pl.pallas_call(
        body,
        out_shape=[shape if keep_out else pltpu.VMEM(shape.shape, shape.dtype) for shape, keep_out in outs],
        in_specs=[SMEM if i in smem else VMEM for i in range(n_in)],
        out_specs=[VMEM] * len(outs),
        scratch_shapes=list(scratch),
        compiler_params=None if free else pltpu.CompilerParams(vmem_limit_bytes=16 * 2**20),
        name=name,
    )

    def apply(*args):
        return run(
            *[
                a if i in smem or i in free else pltpu.with_memory_space_constraint(a, pltpu.VMEM)
                for i, a in enumerate(args)
            ]
        )

    return apply


def held(*shape, dtype=BF16):
    return (jax.ShapeDtypeStruct(shape, dtype), False)


def given(shape, dtype):
    return (jax.ShapeDtypeStruct(shape, dtype), True)


def nt(a, b):
    return lax.dot_general(a, b, (((1,), (1,)), ((), ())), preferred_element_type=F32)


def nn(a, b):
    return jnp.dot(a, b, preferred_element_type=F32)


def put_chunks(scr, value, tensor):
    for r in range(2):
        for k in range(4):
            scr[pl.ds(tensor * 8 + r * 4 + k, 64, stride=16), :] = value[
                r * 64 : (r + 1) * 64, k * LANES : (k + 1) * LANES
            ]


def get_chunks(scr, tensor):
    return jnp.concatenate(
        [
            jnp.concatenate(
                [scr[pl.ds(tensor * 8 + r * 4 + k, 64, stride=16), :] for k in range(4)], axis=1
            )
            for r in range(2)
        ],
        axis=0,
    )


def pack_body(treat_rows, embed, cot, treat_vec, send, scr):
    first = lax.axis_index(CELL) * 2
    vec = treat_vec[...]
    shifted = jnp.concatenate(
        [
            embed[0, r].astype(F32) + treat_rows[0, first + r].astype(F32) * vec
            for r in range(2)
        ],
        axis=0,
    )
    put_chunks(scr, shifted, 0)
    put_chunks(scr, jnp.concatenate([cot[0, 0], cot[0, 1]], axis=0).astype(F32), 1)
    send[...] = scr[...].astype(BF16).reshape(64, 16, LANES)


def unpack_body(recv, out, grad_in, *scr):
    for k in range(4):
        lanes = slice(k * LANES, (k + 1) * LANES)
        part, flat = scr[k], scr[4 + k]
        part[...] = recv[:, 16:, lanes].astype(F32).reshape(256, LANES)
        for x in range(4):
            for y in range(2):
                for m in range(4):
                    flat[pl.ds(m * 64 + x * 16 + y, 8, stride=2), :] = part[
                        pl.ds((2 * x + y) * 4 + m, 8, stride=32), :
                    ]
        for m in range(4):
            ref = out if m < 2 else grad_in
            ref[0, m % 2, :, lanes] = flat[m * 64 : (m + 1) * 64, :].astype(BF16)


def main_body(recv, w_qkv_tall, w_out, bias, send, keep, grads, scr):
    width = w_out.shape[0]
    scale = 1.0 / math.sqrt(width // HEADS)
    scr[...] = recv[...].reshape(1024, LANES).astype(F32)
    shift = get_chunks(scr, 0)
    cot = get_chunks(scr, 1)
    shift_b = shift.astype(BF16)
    cot_b = cot.astype(BF16)
    wq = w_qkv_tall[...]
    wo = w_out[...]
    projected = nn(shift_b, wq).astype(BF16)
    grad_att = nn(cot_b, wo).astype(BF16)
    first = lax.broadcasted_iota(jnp.int32, (128, LANES), 1) < LANES // 2
    zero = jnp.zeros((128, LANES), BF16)
    bias_one = bias[...]
    bias2 = jnp.concatenate([bias_one, bias_one], axis=1)

    def two_heads(slab):
        return jnp.concatenate([jnp.where(first, slab, zero), jnp.where(first, zero, slab)], axis=0)

    def flip(pair):
        return jnp.concatenate([pair[:, :LANES].T, pair[:, LANES:].T], axis=1)

    att, gq, gk, gv = [], [], [], []
    for p in range(width // LANES):
        lo = p * LANES
        q = projected[:, lo : lo + LANES]
        k = projected[:, width + lo : width + lo + LANES]
        v = projected[:, 2 * width + lo : 2 * width + lo + LANES]
        ga = grad_att[:, lo : lo + LANES]
        q2, k2, v2, ga2 = two_heads(q), two_heads(k), two_heads(v), two_heads(ga)
        score = nt(k, q2) + bias2
        grad_prob = nt(v, ga2)
        peak = jnp.max(score, axis=0, keepdims=True)
        exp_score = jnp.exp((score - peak) * scale)
        total = jnp.sum(exp_score, axis=0, keepdims=True)
        prob = exp_score * (1.0 / total)
        prob_b = prob.astype(BF16)
        delta = jnp.sum(prob * grad_prob, axis=0, keepdims=True)
        grad_score = (prob * (grad_prob - delta) * scale).astype(BF16)
        att.append(nn(flip(prob_b), v2).astype(BF16))
        gq.append(nn(flip(grad_score), k2).astype(BF16))
        gk.append(nn(grad_score, q2).astype(BF16))
        gv.append(nn(prob_b, ga2).astype(BF16))
    grad_proj = gq + gk + gv

    mine = lax.axis_index("core") == 0
    tall = [part.T for part in grad_proj] + [
        cot_b[:, k * LANES : (k + 1) * LANES].T for k in range(width // LANES)
    ]
    for n, part in enumerate(tall):
        part = part.reshape(4, 2, 16, LANES)
        even = part[:, 0].reshape(64, LANES)
        odd = part[:, 1].reshape(64, LANES)
        keep[n * 64 : (n + 1) * 64, :] = jnp.where(mine, even, odd)
        send[n * 64 : (n + 1) * 64, :] = jnp.where(mine, odd, even)
    for k in range(width // LANES):
        send[1024 + k * 128 : 1024 + (k + 1) * 128, :] = shift_b[:, k * LANES : (k + 1) * LANES]
        send[1536 + k * 128 : 1536 + (k + 1) * 128, :] = att[k]

    for p, part in enumerate(grad_proj):
        grads[:, p * LANES : (p + 1) * LANES] = part


def rows_body(recv, own, grads, w_qkv_tall, w_out, rows_out, scr):
    width = w_out.shape[0]
    scr[...] = recv[...].reshape(1024, LANES).astype(F32)
    shift = get_chunks(scr, 0)
    cot = get_chunks(scr, 1)
    attended = jnp.concatenate(
        [own[1536 + k * 128 : 1536 + (k + 1) * 128, :] for k in range(width // LANES)], axis=1
    )
    out = shift + nt(attended, w_out[...])
    grad_in = cot + nt(grads[...], w_qkv_tall[...])
    for k in range(width // LANES):
        lanes = slice(k * LANES, (k + 1) * LANES)
        here = scr.at[k * 256 : (k + 1) * 256]
        here[:128, :] = out[:, lanes]
        here[128:, :] = grad_in[:, lanes]
        for x in range(4):
            for y in range(2):
                for m in range(4):
                    rows_out[2 * x + y, m * 8 : (m + 1) * 8, lanes] = here[
                        pl.ds(m * 64 + x * 16 + y, 8, stride=2), :
                    ].astype(BF16)


def weight_body(keep, own, other, rows_out, merged):
    def tokens(base):
        return jnp.concatenate(
            [
                jnp.concatenate(
                    [ref[base + k * 128 : base + (k + 1) * 128, :] for k in range(4)], axis=1
                )
                for ref in (own, other)
            ],
            axis=0,
        )

    left = jnp.concatenate([keep[...], other[:1024, :]], axis=1)
    shift = tokens(1024)
    att = tokens(1536)
    for x in range(4):
        right = shift if x < 3 else att
        block = nn(left[x * 256 : (x + 1) * 256], right).astype(BF16).reshape(8, 2, 16, 512)
        for y in range(2):
            merged[2 * x + y, :128, :] = block[:, y].reshape(128, 512)
            merged[2 * x + y, 128:, :] = rows_out[2 * x + y]


def sum_near_body(parts, out, *scr):
    total = parts[0, :128].astype(F32)
    for n in range(1, 8):
        total = total + parts[n, :128].astype(F32)
    out[:, :16, :] = total.astype(BF16).reshape(8, 16, 512)
    for k, part in enumerate(scr):
        lanes = slice(k * LANES, (k + 1) * LANES)
        for n in range(8):
            for m in range(4):
                part[pl.ds(n * 4 + m, 8, stride=32), :] = parts[
                    n, 128 + m * 8 : 128 + (m + 1) * 8, lanes
                ].astype(F32)
        out[:, 16:, lanes] = part[...].astype(BF16).reshape(8, 32, LANES)


def sum_far_body(parts, out):
    total = parts[0, :16].astype(F32)
    for n in range(1, 8):
        total = total + parts[n, :16].astype(F32)
    total = total.astype(BF16)
    for n in range(8):
        out[n] = total


def sum_z_body(gscale, parts, out):
    for core in range(2):
        total = parts[core].astype(F32)
        for z in range(1, 4):
            total = total + parts[2 * z + core].astype(F32)
        out[core * 16 : (core + 1) * 16, :] = total * gscale


def prep_body(pattern, train, w_qkv, w_out, bias, w_qkv_tall, w_out_here):
    key = lax.broadcasted_iota(jnp.int32, (128, 128), 0)
    query = lax.broadcasted_iota(jnp.int32, (128, 128), 1)
    key_block = lax.rem(key, 64) // 16
    query_block = lax.rem(query, 64) // 16
    open_block = jnp.zeros((128, 128), jnp.int32)
    for a in range(4):
        for b in range(4):
            here = (query_block == a) & (key_block == b)
            open_block = jnp.where(here, pattern[a, b], open_block)
    source = 2 * lax.rem(key, 64) + key // 64
    is_train = jnp.where(query == source, train[...].astype(F32), 0.0)
    is_train = jnp.sum(is_train, axis=1, keepdims=True) == 1.0
    allowed = ((open_block == 1) & is_train) | (key == query)
    bias[...] = jnp.where(allowed, 0.0, -jnp.inf).astype(F32)
    for e in range(w_qkv.shape[0] // LANES):
        w_qkv_tall[:, e * LANES : (e + 1) * LANES] = w_qkv[e * LANES : (e + 1) * LANES, :].T
    w_out_here[...] = w_out[...]


def per_device(row_embed, cotangent, w_qkv, w_out, treat_vec, is_train, treated, block_pattern):
    scr = pltpu.VMEM((1024, LANES), F32)
    rows = row_embed.shape
    (packed,) = call(pack_body, [held(64, 16, LANES)], 4, [scr], (0,), (1, 2, 3), "pack")(
        treated, row_embed, cotangent, treat_vec.reshape(1, -1)
    )
    bias, w_qkv_tall, w_out = call(
        prep_body,
        [
            held(128, 128, dtype=F32),
            held(*w_qkv.shape[::-1]),
            held(*w_out.shape),
        ],
        4,
        smem=(0,),
        free=(1, 2, 3),
        name="prep",
    )(block_pattern, is_train, w_qkv, w_out)
    recv = lax.all_to_all(packed, CELL, 0, 0, tiled=True)
    send, keep, grads = call(
        main_body,
        [held(2048, LANES), held(1024, LANES), held(128, 1536)],
        4,
        [scr],
        name="attend",
    )(recv, w_qkv_tall, w_out, bias)
    other = lax.ppermute(send, "core", [(0, 1), (1, 0)])
    (rows_out,) = call(rows_body, [held(8, 32, 512)], 5, [scr], name="rows")(
        recv, send, grads, w_qkv_tall, w_out
    )
    (merged,) = call(weight_body, [held(8, 160, 512)], 4, name="weight")(
        keep, send, other, rows_out
    )
    by_near = lax.all_to_all(merged, NEAR, 0, 0, tiled=True)
    tall = [pltpu.VMEM((256, LANES), F32)] * 4
    (part_near,) = call(sum_near_body, [held(8, 48, 512)], 1, tall, name="sum_near")(by_near)
    by_far = lax.all_to_all(part_near, FAR, 0, 0, tiled=True)
    (part_far,) = call(sum_far_body, [held(8, 16, 512)], 1, name="sum_far")(by_far)
    by_z = lax.all_to_all(part_far, GRP, 0, 0, tiled=True)
    gscale = 1.0 / math.sqrt(8 * 128 * 64)
    (summed,) = call(
        functools.partial(sum_z_body, gscale), [given((32, 512), F32)], 1, name="sum_z"
    )(by_z)
    out, grad_in = call(
        unpack_body, [given(rows, BF16), given(rows, BF16)], 1, tall * 2, name="unpack"
    )(by_far)
    return out, grad_in, summed


def solution(mesh):
    fine = Mesh(mesh.devices.reshape(4, 2, 4, 2, 4, 2), AXES)
    cells = P(GRP, CELL, None, None)
    return jax.shard_map(
        per_device,
        mesh=fine,
        in_specs=(cells, cells, P(), P(), P(), P(GRP, None), P(GRP, None), P()),
        out_specs=(cells, cells, P(CELL, None)),
        check_vma=False,
    )
```

```python
import functools
import math

import jax
import jax.numpy as jnp
from jax import lax
from jax.experimental import pallas as pl
from jax.experimental.pallas import tpu as pltpu
from jax.sharding import Mesh, PartitionSpec as P

HEADS = 8
BLK = 32
F32 = jnp.float32
BF16 = jnp.bfloat16
AXES = ("z_lo", "core", "x", "z_hi", "y_hi", "y_lo")
GRP = ("z_lo", "core")
CELL = ("x", "z_hi", "y_hi", "y_lo")
NEAR = ("x", "y_lo")
FAR = ("z_hi", "y_hi")
LANES = 128
VMEM = pl.BlockSpec(memory_space=pltpu.VMEM)
SMEM = pl.BlockSpec(memory_space=pltpu.SMEM)


def call(body, outs, n_in, scratch=(), smem=(), free=(), name=None):
    run = pl.pallas_call(
        body,
        out_shape=[shape if keep_out else pltpu.VMEM(shape.shape, shape.dtype) for shape, keep_out in outs],
        in_specs=[SMEM if i in smem else VMEM for i in range(n_in)],
        out_specs=[VMEM] * len(outs),
        scratch_shapes=list(scratch),
        compiler_params=None if free else pltpu.CompilerParams(vmem_limit_bytes=16 * 2**20),
        name=name,
    )

    def apply(*args):
        return run(
            *[
                a if i in smem or i in free else pltpu.with_memory_space_constraint(a, pltpu.VMEM)
                for i, a in enumerate(args)
            ]
        )

    return apply


def held(*shape, dtype=BF16):
    return (jax.ShapeDtypeStruct(shape, dtype), False)


def given(shape, dtype):
    return (jax.ShapeDtypeStruct(shape, dtype), True)


def nt(a, b):
    return lax.dot_general(a, b, (((1,), (1,)), ((), ())), preferred_element_type=F32)


def nn(a, b):
    return jnp.dot(a, b, preferred_element_type=F32)


def put_chunks(scr, value, tensor):
    for r in range(2):
        for k in range(4):
            scr[pl.ds(tensor * 8 + r * 4 + k, 64, stride=16), :] = value[
                r * 64 : (r + 1) * 64, k * LANES : (k + 1) * LANES
            ]


def get_chunks(scr, tensor):
    return jnp.concatenate(
        [
            jnp.concatenate(
                [scr[pl.ds(tensor * 8 + r * 4 + k, 64, stride=16), :] for k in range(4)], axis=1
            )
            for r in range(2)
        ],
        axis=0,
    )


def pack_body(embed, cot, send, scr):
    for n, ref in enumerate((embed, cot)):
        put_chunks(scr, jnp.concatenate([ref[0, 0], ref[0, 1]], axis=0).astype(F32), n)
    send[...] = scr[...].astype(BF16).reshape(64, 16, LANES)


def unpack_body(recv, out, grad_in, *scr):
    for k in range(4):
        lanes = slice(k * LANES, (k + 1) * LANES)
        part, flat = scr[k], scr[4 + k]
        part[...] = recv[:, 16:, lanes].astype(F32).reshape(256, LANES)
        for x in range(4):
            for y in range(2):
                for m in range(4):
                    flat[pl.ds(m * 64 + x * 16 + y, 8, stride=2), :] = part[
                        pl.ds((2 * x + y) * 4 + m, 8, stride=32), :
                    ]
        for m in range(4):
            ref = out if m < 2 else grad_in
            ref[0, m % 2, :, lanes] = flat[m * 64 : (m + 1) * 64, :].astype(BF16)


def main_body(recv, w_qkv_tall, w_out, bias, treatment, send, keep, grads, scr):
    width = w_out.shape[0]
    scale = 1.0 / math.sqrt(width // HEADS)
    scr[...] = recv[...].reshape(1024, LANES).astype(F32)
    shift = get_chunks(scr, 0) + treatment[...]
    cot = get_chunks(scr, 1)
    shift_b = shift.astype(BF16)
    cot_b = cot.astype(BF16)
    wq = w_qkv_tall[...]
    wo = w_out[...]
    projected = nn(shift_b, wq).astype(BF16)
    grad_att = nn(cot_b, wo).astype(BF16)
    first = lax.broadcasted_iota(jnp.int32, (128, LANES), 1) < LANES // 2
    zero = jnp.zeros((128, LANES), BF16)
    bias_one = bias[...]
    bias2 = jnp.concatenate([bias_one, bias_one], axis=1)

    def two_heads(slab):
        return jnp.concatenate([jnp.where(first, slab, zero), jnp.where(first, zero, slab)], axis=0)

    def flip(pair):
        return jnp.concatenate([pair[:, :LANES].T, pair[:, LANES:].T], axis=1)

    att, gq, gk, gv = [], [], [], []
    for p in range(width // LANES):
        lo = p * LANES
        q = projected[:, lo : lo + LANES]
        k = projected[:, width + lo : width + lo + LANES]
        v = projected[:, 2 * width + lo : 2 * width + lo + LANES]
        ga = grad_att[:, lo : lo + LANES]
        q2, k2, v2, ga2 = two_heads(q), two_heads(k), two_heads(v), two_heads(ga)
        score = nt(k, q2) + bias2
        grad_prob = nt(v, ga2)
        peak = jnp.max(score, axis=0, keepdims=True)
        exp_score = jnp.exp((score - peak) * scale)
        total = jnp.sum(exp_score, axis=0, keepdims=True)
        prob = exp_score * (1.0 / total)
        prob_b = prob.astype(BF16)
        delta = jnp.sum(prob * grad_prob, axis=0, keepdims=True)
        grad_score = (prob * (grad_prob - delta) * scale).astype(BF16)
        att.append(nn(flip(prob_b), v2).astype(BF16))
        gq.append(nn(flip(grad_score), k2).astype(BF16))
        gk.append(nn(grad_score, q2).astype(BF16))
        gv.append(nn(prob_b, ga2).astype(BF16))
    grad_proj = gq + gk + gv

    mine = lax.axis_index("core") == 0
    tall = [part.T for part in grad_proj] + [
        cot_b[:, k * LANES : (k + 1) * LANES].T for k in range(width // LANES)
    ]
    for n, part in enumerate(tall):
        part = part.reshape(4, 2, 16, LANES)
        even = part[:, 0].reshape(64, LANES)
        odd = part[:, 1].reshape(64, LANES)
        keep[n * 64 : (n + 1) * 64, :] = jnp.where(mine, even, odd)
        send[n * 64 : (n + 1) * 64, :] = jnp.where(mine, odd, even)
    for k in range(width // LANES):
        send[1024 + k * 128 : 1024 + (k + 1) * 128, :] = shift_b[:, k * LANES : (k + 1) * LANES]
        send[1536 + k * 128 : 1536 + (k + 1) * 128, :] = att[k]

    for p, part in enumerate(grad_proj):
        grads[:, p * LANES : (p + 1) * LANES] = part


def rows_body(recv, own, grads, w_qkv_tall, w_out, rows_out, scr):
    width = w_out.shape[0]
    scr[...] = recv[...].reshape(1024, LANES).astype(F32)
    shift = jnp.concatenate(
        [own[1024 + k * 128 : 1024 + (k + 1) * 128, :] for k in range(width // LANES)], axis=1
    ).astype(F32)
    cot = get_chunks(scr, 1)
    attended = jnp.concatenate(
        [own[1536 + k * 128 : 1536 + (k + 1) * 128, :] for k in range(width // LANES)], axis=1
    )
    out = shift + nt(attended, w_out[...])
    grad_in = cot + nt(grads[...], w_qkv_tall[...])
    for k in range(width // LANES):
        lanes = slice(k * LANES, (k + 1) * LANES)
        here = scr.at[k * 256 : (k + 1) * 256]
        here[:128, :] = out[:, lanes]
        here[128:, :] = grad_in[:, lanes]
        for x in range(4):
            for y in range(2):
                for m in range(4):
                    rows_out[2 * x + y, m * 8 : (m + 1) * 8, lanes] = here[
                        pl.ds(m * 64 + x * 16 + y, 8, stride=2), :
                    ].astype(BF16)


def weight_body(keep, own, other, rows_out, merged):
    def tokens(base):
        return jnp.concatenate(
            [
                jnp.concatenate(
                    [ref[base + k * 128 : base + (k + 1) * 128, :] for k in range(4)], axis=1
                )
                for ref in (own, other)
            ],
            axis=0,
        )

    left = jnp.concatenate([keep[...], other[:1024, :]], axis=1)
    shift = tokens(1024)
    att = tokens(1536)
    for x in range(4):
        right = shift if x < 3 else att
        block = nn(left[x * 256 : (x + 1) * 256], right).astype(BF16).reshape(8, 2, 16, 512)
        for y in range(2):
            merged[2 * x + y, :128, :] = block[:, y].reshape(128, 512)
            merged[2 * x + y, 128:, :] = rows_out[2 * x + y]


def sum_near_body(parts, out, *scr):
    total = parts[0, :128].astype(F32)
    for n in range(1, 8):
        total = total + parts[n, :128].astype(F32)
    out[:, :16, :] = total.astype(BF16).reshape(8, 16, 512)
    for k, part in enumerate(scr):
        lanes = slice(k * LANES, (k + 1) * LANES)
        for n in range(8):
            for m in range(4):
                part[pl.ds(n * 4 + m, 8, stride=32), :] = parts[
                    n, 128 + m * 8 : 128 + (m + 1) * 8, lanes
                ].astype(F32)
        out[:, 16:, lanes] = part[...].astype(BF16).reshape(8, 32, LANES)


def sum_far_body(parts, out):
    total = parts[0, :16].astype(F32)
    for n in range(1, 8):
        total = total + parts[n, :16].astype(F32)
    total = total.astype(BF16)
    for n in range(8):
        out[n] = total


def sum_z_body(gscale, parts, out):
    for core in range(2):
        total = parts[core].astype(F32)
        for z in range(1, 4):
            total = total + parts[2 * z + core].astype(F32)
        out[core * 16 : (core + 1) * 16, :] = total * gscale


def prep_body(pattern, train, treated, treat_vec, w_qkv, w_out, bias, treatment, w_qkv_tall, w_out_here):
    key = lax.broadcasted_iota(jnp.int32, (128, 128), 0)
    query = lax.broadcasted_iota(jnp.int32, (128, 128), 1)
    key_block = lax.rem(key, 64) // 16
    query_block = lax.rem(query, 64) // 16
    open_block = jnp.zeros((128, 128), jnp.int32)
    for a in range(4):
        for b in range(4):
            here = (query_block == a) & (key_block == b)
            open_block = jnp.where(here, pattern[a, b], open_block)
    source = 2 * lax.rem(key, 64) + key // 64

    def column(row):
        picked = jnp.where(query == source, row[...].astype(F32), 0.0)
        return jnp.sum(picked, axis=1, keepdims=True)

    is_train = column(train) == 1.0
    treatment[...] = column(treated) * treat_vec[...]
    allowed = ((open_block == 1) & is_train) | (key == query)
    bias[...] = jnp.where(allowed, 0.0, -jnp.inf).astype(F32)
    for e in range(w_qkv.shape[0] // LANES):
        w_qkv_tall[:, e * LANES : (e + 1) * LANES] = w_qkv[e * LANES : (e + 1) * LANES, :].T
    w_out_here[...] = w_out[...]


def per_device(row_embed, cotangent, w_qkv, w_out, treat_vec, is_train, treated, block_pattern):
    scr = pltpu.VMEM((1024, LANES), F32)
    rows = row_embed.shape
    (packed,) = call(pack_body, [held(64, 16, LANES)], 2, [scr], free=(0, 1), name="pack")(
        row_embed, cotangent
    )
    bias, treatment, w_qkv_tall, w_out = call(
        prep_body,
        [
            held(128, 128, dtype=F32),
            held(128, w_qkv.shape[1], dtype=F32),
            held(*w_qkv.shape[::-1]),
            held(*w_out.shape),
        ],
        6,
        smem=(0,),
        free=(1, 2, 3, 4, 5),
        name="prep",
    )(block_pattern, is_train, treated, treat_vec.reshape(1, -1), w_qkv, w_out)
    recv = lax.all_to_all(packed, CELL, 0, 0, tiled=True)
    send, keep, grads = call(
        main_body,
        [held(2048, LANES), held(1024, LANES), held(128, 1536)],
        5,
        [scr],
        name="attend",
    )(recv, w_qkv_tall, w_out, bias, treatment)
    other = lax.ppermute(send, "core", [(0, 1), (1, 0)])
    (rows_out,) = call(rows_body, [held(8, 32, 512)], 5, [scr], name="rows")(
        recv, send, grads, w_qkv_tall, w_out
    )
    (merged,) = call(weight_body, [held(8, 160, 512)], 4, name="weight")(
        keep, send, other, rows_out
    )
    by_near = lax.all_to_all(merged, NEAR, 0, 0, tiled=True)
    tall = [pltpu.VMEM((256, LANES), F32)] * 4
    (part_near,) = call(sum_near_body, [held(8, 48, 512)], 1, tall, name="sum_near")(by_near)
    by_far = lax.all_to_all(part_near, FAR, 0, 0, tiled=True)
    (part_far,) = call(sum_far_body, [held(8, 16, 512)], 1, name="sum_far")(by_far)
    by_z = lax.all_to_all(part_far, GRP, 0, 0, tiled=True)
    gscale = 1.0 / math.sqrt(8 * 128 * 64)
    (summed,) = call(
        functools.partial(sum_z_body, gscale), [given((32, 512), F32)], 1, name="sum_z"
    )(by_z)
    out, grad_in = call(
        unpack_body, [given(rows, BF16), given(rows, BF16)], 1, tall * 2, name="unpack"
    )(by_far)
    return out, grad_in, summed


def solution(mesh):
    fine = Mesh(mesh.devices.reshape(4, 2, 4, 2, 4, 2), AXES)
    cells = P(GRP, CELL, None, None)
    return jax.shard_map(
        per_device,
        mesh=fine,
        in_specs=(cells, cells, P(), P(), P(), P(GRP, None), P(GRP, None), P()),
        out_specs=(cells, cells, P(CELL, None)),
        check_vma=False,
    )
```

```python
import functools
import math

import jax
import jax.numpy as jnp
from jax import lax
from jax.experimental import pallas as pl
from jax.experimental.pallas import tpu as pltpu
from jax.sharding import Mesh, PartitionSpec as P

HEADS = 8
BLK = 32
F32 = jnp.float32
BF16 = jnp.bfloat16
AXES = ("z_lo", "core", "x", "z_hi", "y_hi", "y_lo")
GRP = ("z_lo", "core")
CELL = ("x", "z_hi", "y_hi", "y_lo")
NEAR = ("x", "y_lo")
FAR = ("z_hi", "y_hi")
LANES = 128
VMEM = pl.BlockSpec(memory_space=pltpu.VMEM)
SMEM = pl.BlockSpec(memory_space=pltpu.SMEM)


def call(body, outs, n_in, scratch=(), smem=(), free=(), name=None):
    run = pl.pallas_call(
        body,
        out_shape=[shape if keep_out else pltpu.VMEM(shape.shape, shape.dtype) for shape, keep_out in outs],
        in_specs=[SMEM if i in smem else VMEM for i in range(n_in)],
        out_specs=[VMEM] * len(outs),
        scratch_shapes=list(scratch),
        compiler_params=None if free else pltpu.CompilerParams(vmem_limit_bytes=16 * 2**20),
        name=name,
    )

    def apply(*args):
        return run(
            *[
                a if i in smem or i in free else pltpu.with_memory_space_constraint(a, pltpu.VMEM)
                for i, a in enumerate(args)
            ]
        )

    return apply


def held(*shape, dtype=BF16):
    return (jax.ShapeDtypeStruct(shape, dtype), False)


def given(shape, dtype):
    return (jax.ShapeDtypeStruct(shape, dtype), True)


def nt(a, b):
    return lax.dot_general(a, b, (((1,), (1,)), ((), ())), preferred_element_type=F32)


def nn(a, b):
    return jnp.dot(a, b, preferred_element_type=F32)


def get_chunks(scr, tensor):
    return jnp.concatenate(
        [
            jnp.concatenate(
                [scr[pl.ds(r * 8 + tensor * 4 + k, 64, stride=16), :] for k in range(4)], axis=1
            )
            for r in range(2)
        ],
        axis=0,
    )


def pack_body(embed, cot, send, scr):
    for n, ref in enumerate((embed, cot)):
        value = ref[0, 0].astype(F32)
        for k in range(4):
            scr[pl.ds(n * 4 + k, 64, stride=8), :] = value[:, k * LANES : (k + 1) * LANES]
    send[...] = scr[...].astype(BF16).reshape(64, 8, LANES)


def unpack_body(recv, out, grad_in, *scr):
    for k in range(4):
        lanes = slice(k * LANES, (k + 1) * LANES)
        part, flat = scr[k], scr[4 + k]
        part[...] = recv[:, 16:, lanes].astype(F32).reshape(256, LANES)
        for x in range(4):
            for y in range(2):
                for m in range(4):
                    flat[pl.ds(m * 64 + x * 16 + y, 8, stride=2), :] = part[
                        pl.ds((2 * x + y) * 4 + m, 8, stride=32), :
                    ]
        for m in range(4):
            ref = out if m < 2 else grad_in
            ref[0, m % 2, :, lanes] = flat[m * 64 : (m + 1) * 64, :].astype(BF16)


def main_body(recv, w_qkv_tall, w_out, bias, treatment, send, keep, grads, scr):
    width = w_out.shape[0]
    scale = 1.0 / math.sqrt(width // HEADS)
    scr[...] = recv[...].reshape(1024, LANES).astype(F32)
    shift = get_chunks(scr, 0) + treatment[...]
    cot = get_chunks(scr, 1)
    shift_b = shift.astype(BF16)
    cot_b = cot.astype(BF16)
    wq = w_qkv_tall[...]
    wo = w_out[...]
    projected = nn(shift_b, wq).astype(BF16)
    grad_att = nn(cot_b, wo).astype(BF16)
    first = lax.broadcasted_iota(jnp.int32, (128, LANES), 1) < LANES // 2
    zero = jnp.zeros((128, LANES), BF16)
    bias_one = bias[...]
    bias2 = jnp.concatenate([bias_one, bias_one], axis=1)

    def two_heads(slab):
        return jnp.concatenate([jnp.where(first, slab, zero), jnp.where(first, zero, slab)], axis=0)

    def flip(pair):
        return jnp.concatenate([pair[:, :LANES].T, pair[:, LANES:].T], axis=1)

    att, gq, gk, gv = [], [], [], []
    for p in range(width // LANES):
        lo = p * LANES
        q = projected[:, lo : lo + LANES]
        k = projected[:, width + lo : width + lo + LANES]
        v = projected[:, 2 * width + lo : 2 * width + lo + LANES]
        ga = grad_att[:, lo : lo + LANES]
        q2, k2, v2, ga2 = two_heads(q), two_heads(k), two_heads(v), two_heads(ga)
        score = nt(k, q2) + bias2
        grad_prob = nt(v, ga2)
        peak = jnp.max(score, axis=0, keepdims=True)
        exp_score = jnp.exp((score - peak) * scale)
        total = jnp.sum(exp_score, axis=0, keepdims=True)
        prob = exp_score * (1.0 / total)
        prob_b = prob.astype(BF16)
        delta = jnp.sum(prob * grad_prob, axis=0, keepdims=True)
        grad_score = (prob * (grad_prob - delta) * scale).astype(BF16)
        att.append(nn(flip(prob_b), v2).astype(BF16))
        gq.append(nn(flip(grad_score), k2).astype(BF16))
        gk.append(nn(grad_score, q2).astype(BF16))
        gv.append(nn(prob_b, ga2).astype(BF16))
    grad_proj = gq + gk + gv

    mine = lax.axis_index("core") == 0
    tall = [part.T for part in grad_proj] + [
        cot_b[:, k * LANES : (k + 1) * LANES].T for k in range(width // LANES)
    ]
    for n, part in enumerate(tall):
        part = part.reshape(4, 2, 16, LANES)
        even = part[:, 0].reshape(64, LANES)
        odd = part[:, 1].reshape(64, LANES)
        keep[n * 64 : (n + 1) * 64, :] = jnp.where(mine, even, odd)
        send[n * 64 : (n + 1) * 64, :] = jnp.where(mine, odd, even)
    for k in range(width // LANES):
        send[1024 + k * 128 : 1024 + (k + 1) * 128, :] = shift_b[:, k * LANES : (k + 1) * LANES]
        send[1536 + k * 128 : 1536 + (k + 1) * 128, :] = att[k]

    for p, part in enumerate(grad_proj):
        grads[:, p * LANES : (p + 1) * LANES] = part


def rows_body(recv, own, grads, w_qkv_tall, w_out, rows_out, scr):
    width = w_out.shape[0]
    scr[...] = recv[...].reshape(1024, LANES).astype(F32)
    shift = jnp.concatenate(
        [own[1024 + k * 128 : 1024 + (k + 1) * 128, :] for k in range(width // LANES)], axis=1
    ).astype(F32)
    cot = get_chunks(scr, 1)
    attended = jnp.concatenate(
        [own[1536 + k * 128 : 1536 + (k + 1) * 128, :] for k in range(width // LANES)], axis=1
    )
    out = shift + nt(attended, w_out[...])
    grad_in = cot + nt(grads[...], w_qkv_tall[...])
    for k in range(width // LANES):
        lanes = slice(k * LANES, (k + 1) * LANES)
        here = scr.at[k * 256 : (k + 1) * 256]
        here[:128, :] = out[:, lanes]
        here[128:, :] = grad_in[:, lanes]
        for x in range(4):
            for y in range(2):
                for m in range(4):
                    rows_out[2 * x + y, m * 8 : (m + 1) * 8, lanes] = here[
                        pl.ds(m * 64 + x * 16 + y, 8, stride=2), :
                    ].astype(BF16)


def weight_body(keep, own, other, rows_out, merged):
    def tokens(base):
        return jnp.concatenate(
            [
                jnp.concatenate(
                    [ref[base + k * 128 : base + (k + 1) * 128, :] for k in range(4)], axis=1
                )
                for ref in (own, other)
            ],
            axis=0,
        )

    left = jnp.concatenate([keep[...], other[:1024, :]], axis=1)
    shift = tokens(1024)
    att = tokens(1536)
    for x in range(4):
        right = shift if x < 3 else att
        block = nn(left[x * 256 : (x + 1) * 256], right).astype(BF16).reshape(8, 2, 16, 512)
        for y in range(2):
            merged[2 * x + y, :128, :] = block[:, y].reshape(128, 512)
            merged[2 * x + y, 128:, :] = rows_out[2 * x + y]


def sum_near_body(parts, out, *scr):
    total = parts[0, :128].astype(F32)
    for n in range(1, 8):
        total = total + parts[n, :128].astype(F32)
    out[:, :16, :] = total.astype(BF16).reshape(8, 16, 512)
    for k, part in enumerate(scr):
        lanes = slice(k * LANES, (k + 1) * LANES)
        for n in range(8):
            for m in range(4):
                part[pl.ds(n * 4 + m, 8, stride=32), :] = parts[
                    n, 128 + m * 8 : 128 + (m + 1) * 8, lanes
                ].astype(F32)
        out[:, 16:, lanes] = part[...].astype(BF16).reshape(8, 32, LANES)


def sum_far_body(parts, out):
    total = parts[0, :16].astype(F32)
    for n in range(1, 8):
        total = total + parts[n, :16].astype(F32)
    total = total.astype(BF16)
    for n in range(8):
        out[n] = total


def sum_z_body(gscale, parts, out):
    for core in range(2):
        total = parts[core].astype(F32)
        for z in range(1, 4):
            total = total + parts[2 * z + core].astype(F32)
        out[core * 16 : (core + 1) * 16, :] = total * gscale


def prep_body(pattern, train, treated, treat_vec, w_qkv, w_out, bias, treatment, w_qkv_tall, w_out_here):
    key = lax.broadcasted_iota(jnp.int32, (128, 128), 0)
    query = lax.broadcasted_iota(jnp.int32, (128, 128), 1)
    key_block = lax.rem(key, 64) // 16
    query_block = lax.rem(query, 64) // 16
    open_block = jnp.zeros((128, 128), jnp.int32)
    for a in range(4):
        for b in range(4):
            here = (query_block == a) & (key_block == b)
            open_block = jnp.where(here, pattern[a, b], open_block)
    source = 2 * lax.rem(key, 64) + key // 64

    def column(row):
        picked = jnp.where(query == source, row[...].astype(F32), 0.0)
        return jnp.sum(picked, axis=1, keepdims=True)

    is_train = column(train) == 1.0
    treatment[...] = column(treated) * treat_vec[...]
    allowed = ((open_block == 1) & is_train) | (key == query)
    bias[...] = jnp.where(allowed, 0.0, -jnp.inf).astype(F32)
    for e in range(w_qkv.shape[0] // LANES):
        w_qkv_tall[:, e * LANES : (e + 1) * LANES] = w_qkv[e * LANES : (e + 1) * LANES, :].T
    w_out_here[...] = w_out[...]


def per_device(row_embed, cotangent, w_qkv, w_out, treat_vec, is_train, treated, block_pattern):
    scr = pltpu.VMEM((1024, LANES), F32)
    rows = row_embed.shape
    row = pl.BlockSpec((1, 1) + rows[2:], lambda r: (0, r, 0, 0))
    packed = pl.pallas_call(
        pack_body,
        grid=(2,),
        out_shape=jax.ShapeDtypeStruct((64, 16, LANES), BF16),
        in_specs=[row, row],
        out_specs=pl.BlockSpec((64, 8, LANES), lambda r: (0, r, 0)),
        scratch_shapes=[pltpu.VMEM((512, LANES), F32)],
        name="pack",
    )(row_embed, cotangent)
    bias, treatment, w_qkv_tall, w_out = call(
        prep_body,
        [
            held(128, 128, dtype=F32),
            held(128, w_qkv.shape[1], dtype=F32),
            held(*w_qkv.shape[::-1]),
            held(*w_out.shape),
        ],
        6,
        smem=(0,),
        free=(1, 2, 3, 4, 5),
        name="prep",
    )(block_pattern, is_train, treated, treat_vec.reshape(1, -1), w_qkv, w_out)
    recv = lax.all_to_all(packed, CELL, 0, 0, tiled=True)
    send, keep, grads = call(
        main_body,
        [held(2048, LANES), held(1024, LANES), held(128, 1536)],
        5,
        [scr],
        name="attend",
    )(recv, w_qkv_tall, w_out, bias, treatment)
    other = lax.ppermute(send, "core", [(0, 1), (1, 0)])
    (rows_out,) = call(rows_body, [held(8, 32, 512)], 5, [scr], name="rows")(
        recv, send, grads, w_qkv_tall, w_out
    )
    (merged,) = call(weight_body, [held(8, 160, 512)], 4, name="weight")(
        keep, send, other, rows_out
    )
    by_near = lax.all_to_all(merged, NEAR, 0, 0, tiled=True)
    tall = [pltpu.VMEM((256, LANES), F32)] * 4
    (part_near,) = call(sum_near_body, [held(8, 48, 512)], 1, tall, name="sum_near")(by_near)
    by_far = lax.all_to_all(part_near, FAR, 0, 0, tiled=True)
    (part_far,) = call(sum_far_body, [held(8, 16, 512)], 1, name="sum_far")(by_far)
    by_z = lax.all_to_all(part_far, GRP, 0, 0, tiled=True)
    gscale = 1.0 / math.sqrt(8 * 128 * 64)
    (summed,) = call(
        functools.partial(sum_z_body, gscale), [given((32, 512), F32)], 1, name="sum_z"
    )(by_z)
    out, grad_in = call(
        unpack_body, [given(rows, BF16), given(rows, BF16)], 1, tall * 2, name="unpack"
    )(by_far)
    return out, grad_in, summed


def solution(mesh):
    fine = Mesh(mesh.devices.reshape(4, 2, 4, 2, 4, 2), AXES)
    cells = P(GRP, CELL, None, None)
    return jax.shard_map(
        per_device,
        mesh=fine,
        in_specs=(cells, cells, P(), P(), P(), P(GRP, None), P(GRP, None), P()),
        out_specs=(cells, cells, P(CELL, None)),
        check_vma=False,
    )
```
